128 devices in a mesh: req: 4 (over z), exp: 32 (over x, y, core).
Axes of the slice: x: 4, y: 4, z: 4, core: 2. Of those that a mesh axis runs over, the one named last changes fastest.
Arguments:
- attn_out: bfloat16 [16384, 2048], P(('req', 'exp')), may hold values from -6 to 6
- residual: bfloat16 [16384, 2048], P(('req', 'exp')), may hold values from -6 to 6
- out_weight: bfloat16 [2048, 2048], P('exp'), may hold values from -0.125 to 0.125
- norm_gain: float32 [2048], replicated, may hold values from 0.25 to 1.75
- expert_ids: int32 [16384, 6], P(('req', 'exp')), may hold values from 0 to 31, all different within a row; in each aligned block of 128 rows (0 to 127, 128 to 255, ...) at most 36 rows name the same one
- gate_weights: float32 [16384, 6], P(('req', 'exp')), may hold values from 0.05 to 0.5
- expert_gate: bfloat16 [32, 2048, 1408], P('exp'), may hold values from -0.125 to 0.125
- expert_up: bfloat16 [32, 2048, 1408], P('exp'), may hold values from -0.125 to 0.125
- expert_down: bfloat16 [32, 1408, 2048], P('exp'), may hold values from -0.15625 to 0.15625
- shared_gate: bfloat16 [2048, 1408], P(None, 'req'), may hold values from -0.125 to 0.125
- shared_up: bfloat16 [2048, 1408], P(None, 'req'), may hold values from -0.125 to 0.125
- shared_down: bfloat16 [2048, 1408], P(None, 'req'), may hold values from -0.15625 to 0.15625
Outputs:
- mixed: bfloat16 [16384, 2048], P(('req', 'exp'))
The draws below stay inside these ranges and needn't reach their ends.
Inputs may be any that keep to these rules, and one draw needn't show every extreme that they name: `expert_ids`: within the rows of one device no expert is named by more than 36 rows, and each row names 6 different experts.
All inputs are finite; a program needn't handle non-finite values.
Results may differ from the reference program's by a relative error of at most 0.012.
Values may be sent and summed in bfloat16 or wider, within the bound.
A program may use at most 192 MiB of HBM per device.

```python
import math
import jax
import jax.numpy as jnp
import numpy as np
from jax import lax

D = 2048
FF = 1408
SHARED_FF = 1408
TOPK = 6
ROWS_DEV = 128
EXPERTS = 32
ROWS = 16384
CAP = 36
N_REQ = 4
N_EXP = 32


def steps_of(stream_key, shape, pieces, smallest, largest):
    level = 1.0
    for axis_at, blocks in pieces:
        steps = jax.random.uniform(jax.random.fold_in(jax.random.fold_in(stream_key, 6), axis_at), (blocks,), jnp.float32, smallest / len(pieces), largest / len(pieces))
        level = level * jnp.repeat(jnp.exp(steps), shape[axis_at] // blocks).reshape((-1,) + (1,) * (len(shape) - 1 - axis_at))
    return level


def shared_out(stream_key, own, number, rows, number_of, top, limit, slope):
    ranking = jax.random.permutation(stream_key, number_of)
    crowded, usual = shares(number_of, rows * top, limit, slope, True), shares(number_of, rows * top, limit, slope, False)
    places = jnp.arange(number_of)

    def named(lengths, rotation):
        used = int((lengths > 0).sum())
        fixed = max(1, used // 4)
        passed = fixed + (places - fixed + rotation * (used - fixed)) % max(1, number_of - fixed)
        return jnp.zeros((number_of,), jnp.int32).at[ranking[jnp.where(places < fixed, places, passed)]].set(jnp.asarray(lengths, jnp.int32))

    lengths = jnp.where(number % 4 == 0, named(crowded, number // 4), named(usual, number - number // 4 - 1))
    mixed = jax.random.permutation(jax.random.fold_in(own, 3), number_of)
    donor, taker = mixed[0:number_of // 2 * 2:2], mixed[1:number_of // 2 * 2:2]
    slack = jnp.minimum(lengths[donor] - 1, limit - lengths[taker]) // 2
    slack = jnp.where((donor == ranking[0]) | (taker == ranking[0]) | (lengths[taker] == 0), 0, jnp.maximum(slack, 0))
    passed = jax.random.randint(jax.random.fold_in(own, 4), (number_of // 2,), 0, 1 << 20) % (slack + 1)
    lengths = lengths.at[donor].add(-passed).at[taker].add(passed)
    members = jnp.searchsorted(jnp.cumsum(lengths), jnp.arange(rows * top), side="right").astype(jnp.int32)
    table = members.reshape(top, rows).T
    table = table[jax.random.permutation(jax.random.fold_in(own, 1), rows)]
    rotation = jax.random.randint(jax.random.fold_in(own, 2), (rows, 1), 0, top)
    return jnp.take_along_axis(table, (jnp.arange(top)[None, :] + rotation) % top, axis=1)


def shares(number_of, total, most, skew, full):
    loads = [(1 << 20) // math.isqrt(rank ** skew) + 1 for rank in range(1, number_of + 1)]
    largest = most if full else min(most, max(-(-total // number_of), total * loads[0] // sum(loads)))
    least = 1 if total - largest >= number_of - 1 else 0
    counts, spare = [largest] + [least] * (number_of - 1), total - largest - least * (number_of - 1)
    while spare > 0:
        candidates = [i for i in range(1, number_of) if counts[i] < largest] or [i for i in range(1, number_of) if counts[i] < most]
        mass, budget = sum([loads[i] for i in candidates]), spare
        for i in candidates:
            addition = min(most - counts[i], max(1, budget * loads[i] // mass), spare)
            counts[i] = counts[i] + addition
            spare = spare - addition
    return np.array(counts)


def scatter_about(own_key, shape, scale, most, shards=(), kind=jnp.bfloat16):
    loudness = steps_of(own_key, shape, shards, -0.22, 0.18) if shards else 1.0
    array = jax.random.normal(own_key, shape, jnp.float32) * scale * loudness
    return jnp.minimum(jnp.maximum(array, -most), most).astype(kind)


def setup_inputs(seed: int = 0) -> dict:
    key_of = jax.random.split(jax.random.key(seed), 13)
    attn_out = scatter_about(key_of[0], (ROWS, D), 1.0, 6.0, ((0, 128),))
    residual = scatter_about(key_of[1], (ROWS, D), 1.0, 6.0, ((0, 128),))
    out_weight = scatter_about(key_of[2], (D, D), D ** -0.5, 0.125, ((0, 32),))
    norm_gain = jnp.clip(1.0 + 0.15 * jax.random.normal(key_of[3], (D,), jnp.float32), 0.25, 1.75)
    expert_ids_keys = jax.random.split(jax.random.fold_in(key_of[4], 1), ROWS // ROWS_DEV)
    expert_ids_turns = jax.random.permutation(jax.random.fold_in(key_of[4], 3), ROWS // ROWS_DEV)
    expert_ids = jax.vmap(lambda own, number: shared_out(jax.random.fold_in(key_of[4], 2), own, number, ROWS_DEV, EXPERTS, TOPK, CAP, 3))(expert_ids_keys, expert_ids_turns).reshape((ROWS, TOPK))
    gate_weights = jnp.clip(0.05 + 0.45 * jax.random.uniform(key_of[5], (ROWS, TOPK), jnp.float32) ** steps_of(key_of[5], (ROWS, TOPK), ((0, 128),), -0.2, 0.2), 0.05, 0.5)
    expert_gate = scatter_about(key_of[6], (EXPERTS, D, FF), D ** -0.5, 0.125, ((0, 32),))
    expert_up = scatter_about(key_of[7], (EXPERTS, D, FF), D ** -0.5, 0.125, ((0, 32),))
    expert_down = scatter_about(key_of[8], (EXPERTS, FF, D), FF ** -0.5, 0.15625, ((0, 32),))
    shared_gate = scatter_about(key_of[9], (D, SHARED_FF), D ** -0.5, 0.125, ((1, 4),))
    shared_up = scatter_about(key_of[10], (D, SHARED_FF), D ** -0.5, 0.125, ((1, 4),))
    shared_down = scatter_about(key_of[11], (D, SHARED_FF), SHARED_FF ** -0.5, 0.15625, ((1, 4),))
    return dict(attn_out=attn_out, residual=residual, out_weight=out_weight, norm_gain=norm_gain, expert_ids=expert_ids, gate_weights=gate_weights, expert_gate=expert_gate, expert_up=expert_up, expert_down=expert_down, shared_gate=shared_gate, shared_up=shared_up, shared_down=shared_down)


def reference(attn_out, residual, out_weight, norm_gain, expert_ids, gate_weights, expert_gate, expert_up, expert_down, shared_gate, shared_up, shared_down):
    proj = jnp.dot(attn_out, out_weight, preferred_element_type=jnp.float32)
    stream = (residual.astype(jnp.float32) + proj).astype(jnp.bfloat16)
    stream_f = stream.astype(jnp.float32)
    scale = lax.rsqrt(lax.optimization_barrier(jnp.mean(stream_f * stream_f, axis=1, keepdims=True)) + 1e-06)
    normed = (stream_f * scale * norm_gain).astype(jnp.bfloat16)
    shared_g = jnp.dot(normed, shared_gate, preferred_element_type=jnp.float32)
    shared_u = jnp.dot(normed, shared_up, preferred_element_type=jnp.float32)
    shared_hidden = (jax.nn.silu(shared_g) * shared_u).astype(jnp.bfloat16)
    shared = lax.dot_general(shared_hidden, shared_down, (((1,), (1,)), ((), ())), preferred_element_type=jnp.float32)
    flat_ids = expert_ids.reshape(-1).astype(jnp.int32)
    weights = gate_weights.reshape(-1)
    pairs = ROWS * TOPK
    room = CAP * N_REQ * N_EXP
    pair_index = jnp.arange(pairs, dtype=jnp.int32)

    def one_expert(total, inputs):
        w_gate, w_up, w_down, which = inputs
        hit = flat_ids == which
        position = (jnp.cumsum(hit.astype(jnp.int32)) - 1).astype(jnp.int32)
        target = jnp.where(hit, position, room).astype(jnp.int32)
        table = jnp.full((room,), pairs, jnp.int32).at[target].set(pair_index, mode='drop')
        valid = table < pairs
        safe_pair = jnp.minimum(table, pairs - 1).astype(jnp.int32)
        row_index = (safe_pair // TOPK).astype(jnp.int32)
        taken = normed[row_index]
        gate_part = jnp.dot(taken, w_gate, preferred_element_type=jnp.float32)
        up_part = jnp.dot(taken, w_up, preferred_element_type=jnp.float32)
        hidden = (jax.nn.silu(gate_part) * up_part).astype(jnp.bfloat16)
        result = jnp.dot(hidden, w_down, preferred_element_type=jnp.float32).astype(jnp.bfloat16)
        factor = jnp.where(valid, weights[safe_pair], jnp.zeros((), weights.dtype))
        contrib = result.astype(jnp.float32) * factor[:, None]
        return (total.at[row_index].add(contrib), None)
    start_total = jnp.zeros((ROWS, D), jnp.float32)
    routed, _ = lax.scan(one_expert, start_total, (expert_gate, expert_up, expert_down, jnp.arange(EXPERTS, dtype=jnp.int32)))
    return (stream.astype(jnp.float32) + routed + shared).astype(jnp.bfloat16)
```

```python
import jax
import jax.numpy as jnp
from jax import lax
from jax.sharding import PartitionSpec as P


def body(
    attn_out,
    residual,
    out_weight,
    norm_gain,
    expert_ids,
    gate_weights,
    expert_gate,
    expert_up,
    expert_down,
    shared_gate,
    shared_up,
    shared_down,
):
    row_count, width = attn_out.shape
    topk = expert_ids.shape[1]
    experts = lax.axis_size("exp")
    capacity = min(row_count, 3 * row_count * topk // (2 * experts))
    proj = jnp.dot(
        attn_out,
        lax.all_gather(out_weight, "exp", axis=0, tiled=True),
        preferred_element_type=jnp.float32,
    )
    stream = (residual.astype(jnp.float32) + proj).astype(jnp.bfloat16)
    stream_f = stream.astype(jnp.float32)
    scale = lax.rsqrt(jnp.mean(stream_f * stream_f, axis=1, keepdims=True) + 1e-06)
    normed = (stream_f * scale * norm_gain).astype(jnp.bfloat16)

    flat_ids = expert_ids.reshape(-1)
    onehot = (flat_ids[:, None] == jnp.arange(experts, dtype=jnp.int32)[None, :]).astype(jnp.int32)
    position = jnp.sum(jnp.cumsum(onehot, axis=0) * onehot, axis=1) - 1
    slot = flat_ids * capacity + position
    source_row = jnp.arange(row_count * topk, dtype=jnp.int32) // topk
    table = jnp.full((experts * capacity,), row_count, jnp.int32).at[slot].set(source_row)
    rows = jnp.arange(row_count, dtype=jnp.int32)
    pick = (table.reshape(experts, capacity)[:, :, None] == rows[None, None, :]).astype(jnp.bfloat16)
    outgoing = jnp.einsum(
        "ecr,rd->ecd", pick, normed, preferred_element_type=jnp.float32
    ).astype(jnp.bfloat16)
    joined = lax.all_to_all(outgoing, "exp", split_axis=0, concat_axis=0, tiled=True)
    gate_part = jnp.einsum("scd,df->scf", joined, expert_gate[0], preferred_element_type=jnp.float32)
    up_part = jnp.einsum("scd,df->scf", joined, expert_up[0], preferred_element_type=jnp.float32)
    hidden = (jax.nn.silu(gate_part) * up_part).astype(jnp.bfloat16)
    hidden = lax.optimization_barrier(hidden)
    result = jnp.einsum(
        "scf,fd->scd", hidden, expert_down[0], preferred_element_type=jnp.float32
    ).astype(jnp.bfloat16)
    returned = lax.all_to_all(result, "exp", split_axis=0, concat_axis=0, tiled=True)
    slot_weight = jnp.zeros((experts * capacity,), jnp.float32).at[slot].set(gate_weights.reshape(-1))
    combine = jnp.where(
        table.reshape(experts, capacity)[None, :, :] == rows[:, None, None],
        slot_weight.reshape(experts, capacity)[None, :, :],
        0.0,
    )
    routed = jnp.einsum(
        "rec,ecd->rd",
        combine,
        returned.astype(jnp.float32),
        precision=lax.Precision.HIGHEST,
        preferred_element_type=jnp.float32,
    )

    group_rows = lax.all_gather(normed, "req", axis=0, tiled=True)
    s_gate = jnp.dot(group_rows, shared_gate, preferred_element_type=jnp.float32)
    s_up = jnp.dot(group_rows, shared_up, preferred_element_type=jnp.float32)
    s_hidden = (jax.nn.silu(s_gate) * s_up).astype(jnp.bfloat16)
    s_partial = lax.dot_general(
        s_hidden, shared_down, (((1,), (1,)), ((), ())), preferred_element_type=jnp.float32
    )
    shared = lax.psum_scatter(s_partial, "req", scatter_dimension=0, tiled=True)
    return (stream_f + routed + shared).astype(jnp.bfloat16)


def solution(mesh):
    return jax.shard_map(
        body,
        mesh=mesh,
        in_specs=(
            P(("req", "exp"), None),
            P(("req", "exp"), None),
            P("exp", None),
            P(),
            P(("req", "exp"), None),
            P(("req", "exp"), None),
            P("exp", None, None),
            P("exp", None, None),
            P("exp", None, None),
            P(None, "req"),
            P(None, "req"),
            P(None, "req"),
        ),
        out_specs=P(("req", "exp"), None),
        check_vma=False,
    )
```

```python
import jax
import jax.numpy as jnp
from jax import lax
from jax.sharding import PartitionSpec as P


def body(
    attn_out,
    residual,
    out_weight,
    norm_gain,
    expert_ids,
    gate_weights,
    expert_gate,
    expert_up,
    expert_down,
    shared_gate,
    shared_up,
    shared_down,
):
    row_count, width = attn_out.shape
    topk = expert_ids.shape[1]
    experts = lax.axis_size("exp")
    capacity = min(row_count, 3 * row_count * topk // (2 * experts))
    proj = jnp.dot(
        attn_out,
        lax.all_gather(out_weight, "exp", axis=0, tiled=True),
        preferred_element_type=jnp.float32,
    )
    stream = (residual.astype(jnp.float32) + proj).astype(jnp.bfloat16)
    stream_f = stream.astype(jnp.float32)
    scale = lax.rsqrt(jnp.mean(stream_f * stream_f, axis=1, keepdims=True) + 1e-06)
    normed = (stream_f * scale * norm_gain).astype(jnp.bfloat16)

    flat_ids = expert_ids.reshape(-1)
    onehot = (flat_ids[:, None] == jnp.arange(experts, dtype=jnp.int32)[None, :]).astype(jnp.int32)
    position = jnp.sum(jnp.cumsum(onehot, axis=0) * onehot, axis=1) - 1
    slot = flat_ids * capacity + position
    source_row = jnp.arange(row_count * topk, dtype=jnp.int32) // topk
    table = jnp.full((experts * capacity,), row_count, jnp.int32).at[slot].set(source_row)
    rows = jnp.arange(row_count, dtype=jnp.int32)
    pick = (table.reshape(experts, capacity)[:, :, None] == rows[None, None, :]).astype(jnp.bfloat16)
    lanes = 128
    blocks = width // lanes
    outgoing = jnp.einsum(
        "ecr,rjk->ecjk", pick, normed.reshape(row_count, blocks, lanes),
        preferred_element_type=jnp.float32,
    ).astype(jnp.bfloat16)
    joined = lax.all_to_all(
        outgoing.reshape(experts, capacity * blocks, lanes), "exp",
        split_axis=0, concat_axis=0, tiled=True,
    ).reshape(experts, capacity, blocks, lanes)
    gate_w = expert_gate[0].reshape(blocks, lanes, -1)
    up_w = expert_up[0].reshape(blocks, lanes, -1)
    gate_part = jnp.einsum("scjk,jkf->scf", joined, gate_w, preferred_element_type=jnp.float32)
    up_part = jnp.einsum("scjk,jkf->scf", joined, up_w, preferred_element_type=jnp.float32)
    hidden = (jax.nn.silu(gate_part) * up_part).astype(jnp.bfloat16)
    hidden = lax.optimization_barrier(hidden)
    result = jnp.einsum(
        "scf,fjk->scjk", hidden, expert_down[0].reshape(-1, blocks, lanes),
        preferred_element_type=jnp.float32,
    ).astype(jnp.bfloat16)
    returned = lax.all_to_all(
        result.reshape(experts, capacity * blocks, lanes), "exp",
        split_axis=0, concat_axis=0, tiled=True,
    ).reshape(experts, capacity, blocks, lanes)
    slot_weight = jnp.zeros((experts * capacity,), jnp.float32).at[slot].set(gate_weights.reshape(-1))
    combine = jnp.where(
        table.reshape(experts, capacity)[None, :, :] == rows[:, None, None],
        slot_weight.reshape(experts, capacity)[None, :, :],
        0.0,
    )
    routed = jnp.einsum(
        "rec,ecjk->rjk",
        combine,
        returned.astype(jnp.float32),
        precision=lax.Precision.HIGHEST,
        preferred_element_type=jnp.float32,
    ).reshape(row_count, width)

    group_rows = lax.all_gather(normed, "req", axis=0, tiled=True)
    s_gate = jnp.dot(group_rows, shared_gate, preferred_element_type=jnp.float32)
    s_up = jnp.dot(group_rows, shared_up, preferred_element_type=jnp.float32)
    s_hidden = (jax.nn.silu(s_gate) * s_up).astype(jnp.bfloat16)
    s_partial = lax.dot_general(
        s_hidden, shared_down, (((1,), (1,)), ((), ())), preferred_element_type=jnp.float32
    )
    shared = lax.psum_scatter(s_partial, "req", scatter_dimension=0, tiled=True)
    return (stream_f + routed + shared).astype(jnp.bfloat16)


def solution(mesh):
    return jax.shard_map(
        body,
        mesh=mesh,
        in_specs=(
            P(("req", "exp"), None),
            P(("req", "exp"), None),
            P("exp", None),
            P(),
            P(("req", "exp"), None),
            P(("req", "exp"), None),
            P("exp", None, None),
            P("exp", None, None),
            P("exp", None, None),
            P(None, "req"),
            P(None, "req"),
            P(None, "req"),
        ),
        out_specs=P(("req", "exp"), None),
        check_vma=False,
    )
```

```python
import jax
import jax.numpy as jnp
from jax import lax
from jax.sharding import PartitionSpec as P


def body(
    attn_out,
    residual,
    out_weight,
    norm_gain,
    expert_ids,
    gate_weights,
    expert_gate,
    expert_up,
    expert_down,
    shared_gate,
    shared_up,
    shared_down,
):
    row_count, width = attn_out.shape
    topk = expert_ids.shape[1]
    experts = lax.axis_size("exp")
    capacity = min(row_count, 3 * row_count * topk // (2 * experts))
    req = lax.axis_size("req")
    quarter = out_weight.shape[0] // req
    piece = lax.dynamic_slice_in_dim(out_weight, lax.axis_index("req") * quarter, quarter, 0)
    proj = jnp.dot(
        attn_out,
        lax.all_gather(piece, ("exp", "req"), axis=0, tiled=True),
        preferred_element_type=jnp.float32,
    )
    stream = (residual.astype(jnp.float32) + proj).astype(jnp.bfloat16)
    stream_f = stream.astype(jnp.float32)
    scale = lax.rsqrt(jnp.mean(stream_f * stream_f, axis=1, keepdims=True) + 1e-06)
    normed = (stream_f * scale * norm_gain).astype(jnp.bfloat16)

    flat_ids = expert_ids.reshape(-1)
    onehot = (flat_ids[:, None] == jnp.arange(experts, dtype=jnp.int32)[None, :]).astype(jnp.int32)
    position = jnp.sum(jnp.cumsum(onehot, axis=0) * onehot, axis=1) - 1
    slot = flat_ids * capacity + position
    source_row = jnp.arange(row_count * topk, dtype=jnp.int32) // topk
    table = jnp.full((experts * capacity,), row_count, jnp.int32).at[slot].set(source_row)
    rows = jnp.arange(row_count, dtype=jnp.int32)
    pick = (table.reshape(experts, capacity)[:, :, None] == rows[None, None, :]).astype(jnp.bfloat16)
    outgoing = jnp.einsum(
        "ecr,rd->ecd", pick, normed, preferred_element_type=jnp.float32
    ).astype(jnp.bfloat16)
    joined = lax.all_to_all(outgoing, "exp", split_axis=0, concat_axis=0, tiled=True)
    gate_part = jnp.einsum("scd,df->scf", joined, expert_gate[0], preferred_element_type=jnp.float32)
    up_part = jnp.einsum("scd,df->scf", joined, expert_up[0], preferred_element_type=jnp.float32)
    hidden = (jax.nn.silu(gate_part) * up_part).astype(jnp.bfloat16)
    hidden = lax.optimization_barrier(hidden)
    result = jnp.einsum(
        "scf,fd->scd", hidden, expert_down[0], preferred_element_type=jnp.float32
    ).astype(jnp.bfloat16)
    returned = lax.all_to_all(result, "exp", split_axis=0, concat_axis=0, tiled=True)
    slot_weight = jnp.zeros((experts * capacity,), jnp.float32).at[slot].set(gate_weights.reshape(-1))
    combine = jnp.where(
        table.reshape(experts, capacity)[None, :, :] == rows[:, None, None],
        slot_weight.reshape(experts, capacity)[None, :, :],
        0.0,
    )
    routed = jnp.einsum(
        "rec,ecd->rd",
        combine,
        returned.astype(jnp.float32),
        precision=lax.Precision.HIGHEST,
        preferred_element_type=jnp.float32,
    )

    group_rows = lax.all_gather(normed, "req", axis=0, tiled=True)
    s_gate = jnp.dot(group_rows, shared_gate, preferred_element_type=jnp.float32)
    s_up = jnp.dot(group_rows, shared_up, preferred_element_type=jnp.float32)
    s_hidden = (jax.nn.silu(s_gate) * s_up).astype(jnp.bfloat16)
    s_partial = lax.dot_general(
        s_hidden, shared_down, (((1,), (1,)), ((), ())), preferred_element_type=jnp.float32
    )
    shared = lax.psum_scatter(s_partial, "req", scatter_dimension=0, tiled=True)
    return (stream_f + routed + shared).astype(jnp.bfloat16)


def solution(mesh):
    return jax.shard_map(
        body,
        mesh=mesh,
        in_specs=(
            P(("req", "exp"), None),
            P(("req", "exp"), None),
            P("exp", None),
            P(),
            P(("req", "exp"), None),
            P(("req", "exp"), None),
            P("exp", None, None),
            P("exp", None, None),
            P("exp", None, None),
            P(None, "req"),
            P(None, "req"),
            P(None, "req"),
        ),
        out_specs=P(("req", "exp"), None),
        check_vma=False,
    )
```

```python
import jax
import jax.numpy as jnp
from jax import lax
from jax.sharding import PartitionSpec as P


def body(
    attn_out,
    residual,
    out_weight,
    norm_gain,
    expert_ids,
    gate_weights,
    expert_gate,
    expert_up,
    expert_down,
    shared_gate,
    shared_up,
    shared_down,
):
    row_count, width = attn_out.shape
    topk = expert_ids.shape[1]
    experts = lax.axis_size("exp")
    capacity = min(row_count, 3 * row_count * topk // (2 * experts))
    proj = jnp.dot(
        attn_out,
        lax.all_gather(out_weight, "exp", axis=0, tiled=True),
        preferred_element_type=jnp.float32,
    )
    stream = (residual.astype(jnp.float32) + proj).astype(jnp.bfloat16)
    stream_f = stream.astype(jnp.float32)
    scale = lax.rsqrt(jnp.mean(stream_f * stream_f, axis=1, keepdims=True) + 1e-06)
    normed = (stream_f * scale * norm_gain).astype(jnp.bfloat16)

    flat_ids = expert_ids.reshape(-1)
    onehot = (flat_ids[:, None] == jnp.arange(experts, dtype=jnp.int32)[None, :]).astype(jnp.int32)
    position = jnp.sum(jnp.cumsum(onehot, axis=0) * onehot, axis=1) - 1
    slot = flat_ids * capacity + position
    source_row = jnp.arange(row_count * topk, dtype=jnp.int32) // topk
    table = jnp.full((experts * capacity,), row_count, jnp.int32).at[slot].set(source_row)
    rows = jnp.arange(row_count, dtype=jnp.int32)
    pick = (table.reshape(experts, capacity)[:, :, None] == rows[None, None, :]).astype(jnp.bfloat16)
    half = width // 2
    joined = []
    for part in range(2):
        cols = normed[:, part * half:(part + 1) * half]
        outgoing = jnp.einsum(
            "ecr,rd->ecd", pick, cols, preferred_element_type=jnp.float32
        ).astype(jnp.bfloat16)
        joined.append(lax.all_to_all(outgoing, "exp", split_axis=0, concat_axis=0, tiled=True))
    w_gate, w_up, w_down = expert_gate[0], expert_up[0], expert_down[0]
    gate_part = sum(
        jnp.einsum("scd,df->scf", joined[p], w_gate[p * half:(p + 1) * half],
                   preferred_element_type=jnp.float32)
        for p in range(2)
    )
    up_part = sum(
        jnp.einsum("scd,df->scf", joined[p], w_up[p * half:(p + 1) * half],
                   preferred_element_type=jnp.float32)
        for p in range(2)
    )
    hidden = (jax.nn.silu(gate_part) * up_part).astype(jnp.bfloat16)
    returned = []
    for part in range(2):
        result = jnp.einsum(
            "scf,fd->scd", hidden, w_down[:, part * half:(part + 1) * half],
            preferred_element_type=jnp.float32,
        ).astype(jnp.bfloat16)
        returned.append(lax.all_to_all(result, "exp", split_axis=0, concat_axis=0, tiled=True))
    slot_weight = jnp.zeros((experts * capacity,), jnp.float32).at[slot].set(gate_weights.reshape(-1))
    combine = jnp.where(
        table.reshape(experts, capacity)[None, :, :] == rows[:, None, None],
        slot_weight.reshape(experts, capacity)[None, :, :],
        0.0,
    )
    routed = jnp.concatenate([
        jnp.einsum(
            "rec,ecd->rd",
            combine,
            returned[p].astype(jnp.float32),
            precision=lax.Precision.HIGHEST,
            preferred_element_type=jnp.float32,
        )
        for p in range(2)
    ], axis=1)

    group_rows = lax.all_gather(normed, "req", axis=0, tiled=True)
    s_gate = jnp.dot(group_rows, shared_gate, preferred_element_type=jnp.float32)
    s_up = jnp.dot(group_rows, shared_up, preferred_element_type=jnp.float32)
    s_hidden = (jax.nn.silu(s_gate) * s_up).astype(jnp.bfloat16)
    s_partial = lax.dot_general(
        s_hidden, shared_down, (((1,), (1,)), ((), ())), preferred_element_type=jnp.float32
    )
    shared = lax.psum_scatter(s_partial, "req", scatter_dimension=0, tiled=True)
    return (stream_f + routed + shared).astype(jnp.bfloat16)


def solution(mesh):
    return jax.shard_map(
        body,
        mesh=mesh,
        in_specs=(
            P(("req", "exp"), None),
            P(("req", "exp"), None),
            P("exp", None),
            P(),
            P(("req", "exp"), None),
            P(("req", "exp"), None),
            P("exp", None, None),
            P("exp", None, None),
            P("exp", None, None),
            P(None, "req"),
            P(None, "req"),
            P(None, "req"),
        ),
        out_specs=P(("req", "exp"), None),
        check_vma=False,
    )
```

```python
import jax
import jax.numpy as jnp
from jax import lax
from jax.sharding import PartitionSpec as P
from jax.experimental import pallas as pl
from jax.experimental.pallas import tpu as pltpu


def _exchange_kernel(x_hbm, o_hbm, send_sems, recv_sems, local_sem):
    n = lax.axis_size("exp")
    me = lax.axis_index("exp")
    grp = lax.axis_index("req")
    mesh_id = pl.DeviceIdType.MESH
    barrier = pltpu.get_barrier_semaphore()
    for k in range(1, n):
        pl.semaphore_signal(barrier, 1, device_id=(grp, lax.rem(me + k, n)), device_id_type=mesh_id)
    pl.semaphore_wait(barrier, n - 1)
    local = pltpu.make_async_copy(x_hbm.at[me], o_hbm.at[me], local_sem)
    local.start()
    copies = []
    for k in range(1, n):
        dest = lax.rem(me + k, n)
        copy = pltpu.make_async_remote_copy(
            src_ref=x_hbm.at[dest],
            dst_ref=o_hbm.at[me],
            send_sem=send_sems.at[k],
            recv_sem=recv_sems.at[k],
            device_id=(grp, dest),
            device_id_type=mesh_id,
        )
        copy.start()
        copies.append(copy)
    for copy in copies:
        copy.wait()
    local.wait()


def exchange(x, collective_id):
    n = x.shape[0]
    return pl.pallas_call(
        _exchange_kernel,
        out_shape=jax.ShapeDtypeStruct(x.shape, x.dtype),
        in_specs=[pl.BlockSpec(memory_space=pl.ANY)],
        out_specs=pl.BlockSpec(memory_space=pl.ANY),
        scratch_shapes=[
            pltpu.SemaphoreType.DMA((n,)),
            pltpu.SemaphoreType.DMA((n,)),
            pltpu.SemaphoreType.DMA,
        ],
        compiler_params=pltpu.CompilerParams(collective_id=collective_id, has_side_effects=True),
    )(x)


def body(
    attn_out,
    residual,
    out_weight,
    norm_gain,
    expert_ids,
    gate_weights,
    expert_gate,
    expert_up,
    expert_down,
    shared_gate,
    shared_up,
    shared_down,
):
    row_count, width = attn_out.shape
    topk = expert_ids.shape[1]
    experts = lax.axis_size("exp")
    capacity = min(row_count, 3 * row_count * topk // (2 * experts))
    proj = jnp.dot(
        attn_out,
        lax.all_gather(out_weight, "exp", axis=0, tiled=True),
        preferred_element_type=jnp.float32,
    )
    stream = (residual.astype(jnp.float32) + proj).astype(jnp.bfloat16)
    stream_f = stream.astype(jnp.float32)
    scale = lax.rsqrt(jnp.mean(stream_f * stream_f, axis=1, keepdims=True) + 1e-06)
    normed = (stream_f * scale * norm_gain).astype(jnp.bfloat16)

    flat_ids = expert_ids.reshape(-1)
    onehot = (flat_ids[:, None] == jnp.arange(experts, dtype=jnp.int32)[None, :]).astype(jnp.int32)
    position = jnp.sum(jnp.cumsum(onehot, axis=0) * onehot, axis=1) - 1
    slot = flat_ids * capacity + position
    source_row = jnp.arange(row_count * topk, dtype=jnp.int32) // topk
    table = jnp.full((experts * capacity,), row_count, jnp.int32).at[slot].set(source_row)
    rows = jnp.arange(row_count, dtype=jnp.int32)
    pick = (table.reshape(experts, capacity)[:, :, None] == rows[None, None, :]).astype(jnp.bfloat16)
    outgoing = jnp.einsum(
        "ecr,rd->ecd", pick, normed, preferred_element_type=jnp.float32
    ).astype(jnp.bfloat16)
    joined = exchange(outgoing, 0)
    gate_part = jnp.einsum("scd,df->scf", joined, expert_gate[0], preferred_element_type=jnp.float32)
    up_part = jnp.einsum("scd,df->scf", joined, expert_up[0], preferred_element_type=jnp.float32)
    hidden = (jax.nn.silu(gate_part) * up_part).astype(jnp.bfloat16)
    hidden = lax.optimization_barrier(hidden)
    result = jnp.einsum(
        "scf,fd->scd", hidden, expert_down[0], preferred_element_type=jnp.float32
    ).astype(jnp.bfloat16)
    returned = exchange(result, 1)
    slot_weight = jnp.zeros((experts * capacity,), jnp.float32).at[slot].set(gate_weights.reshape(-1))
    combine = jnp.where(
        table.reshape(experts, capacity)[None, :, :] == rows[:, None, None],
        slot_weight.reshape(experts, capacity)[None, :, :],
        0.0,
    )
    routed = jnp.einsum(
        "rec,ecd->rd",
        combine,
        returned.astype(jnp.float32),
        precision=lax.Precision.HIGHEST,
        preferred_element_type=jnp.float32,
    )

    group_rows = lax.all_gather(normed, "req", axis=0, tiled=True)
    s_gate = jnp.dot(group_rows, shared_gate, preferred_element_type=jnp.float32)
    s_up = jnp.dot(group_rows, shared_up, preferred_element_type=jnp.float32)
    s_hidden = (jax.nn.silu(s_gate) * s_up).astype(jnp.bfloat16)
    s_partial = lax.dot_general(
        s_hidden, shared_down, (((1,), (1,)), ((), ())), preferred_element_type=jnp.float32
    )
    shared = lax.psum_scatter(s_partial, "req", scatter_dimension=0, tiled=True)
    return (stream_f + routed + shared).astype(jnp.bfloat16)


def solution(mesh):
    return jax.shard_map(
        body,
        mesh=mesh,
        in_specs=(
            P(("req", "exp"), None),
            P(("req", "exp"), None),
            P("exp", None),
            P(),
            P(("req", "exp"), None),
            P(("req", "exp"), None),
            P("exp", None, None),
            P("exp", None, None),
            P("exp", None, None),
            P(None, "req"),
            P(None, "req"),
            P(None, "req"),
        ),
        out_specs=P(("req", "exp"), None),
        check_vma=False,
    )
```

```python
import jax
import jax.numpy as jnp
from jax import lax
from jax.sharding import PartitionSpec as P


def body(
    attn_out,
    residual,
    out_weight,
    norm_gain,
    expert_ids,
    gate_weights,
    expert_gate,
    expert_up,
    expert_down,
    shared_gate,
    shared_up,
    shared_down,
):
    row_count, width = attn_out.shape
    topk = expert_ids.shape[1]
    experts = lax.axis_size("exp")
    capacity = min(row_count, 3 * row_count * topk // (2 * experts))
    proj = jnp.dot(
        attn_out,
        lax.all_gather(out_weight, "exp", axis=0, tiled=True),
        preferred_element_type=jnp.float32,
    )
    stream = (residual.astype(jnp.float32) + proj).astype(jnp.bfloat16)
    stream_f = stream.astype(jnp.float32)
    scale = lax.rsqrt(jnp.mean(stream_f * stream_f, axis=1, keepdims=True) + 1e-06)
    normed = (stream_f * scale * norm_gain).astype(jnp.bfloat16)

    flat_ids = expert_ids.reshape(-1)
    onehot = (flat_ids[:, None] == jnp.arange(experts, dtype=jnp.int32)[None, :]).astype(jnp.int32)
    position = jnp.sum(jnp.cumsum(onehot, axis=0) * onehot, axis=1) - 1
    slot = flat_ids * capacity + position
    source_row = jnp.arange(row_count * topk, dtype=jnp.int32) // topk
    table = jnp.full((experts * capacity,), row_count, jnp.int32).at[slot].set(source_row)
    rows = jnp.arange(row_count, dtype=jnp.int32)
    pick = (table.reshape(experts, capacity)[:, :, None] == rows[None, None, :]).astype(jnp.bfloat16)
    w_gate, w_up, w_down = expert_gate[0], expert_up[0], expert_down[0]
    bounds = [0, min(16, capacity), capacity] if capacity > 16 else [0, capacity]
    returned = []
    for lo, hi in zip(bounds[:-1], bounds[1:]):
        outgoing = jnp.einsum(
            "ecr,rd->ecd", pick[:, lo:hi], normed, preferred_element_type=jnp.float32
        ).astype(jnp.bfloat16)
        joined = lax.all_to_all(outgoing, "exp", split_axis=0, concat_axis=0, tiled=True)
        gate_part = jnp.einsum("scd,df->scf", joined, w_gate, preferred_element_type=jnp.float32)
        up_part = jnp.einsum("scd,df->scf", joined, w_up, preferred_element_type=jnp.float32)
        hidden = (jax.nn.silu(gate_part) * up_part).astype(jnp.bfloat16)
        result = jnp.einsum(
            "scf,fd->scd", hidden, w_down, preferred_element_type=jnp.float32
        ).astype(jnp.bfloat16)
        returned.append(lax.all_to_all(result, "exp", split_axis=0, concat_axis=0, tiled=True))
    slot_weight = jnp.zeros((experts * capacity,), jnp.float32).at[slot].set(gate_weights.reshape(-1))
    combine = jnp.where(
        table.reshape(experts, capacity)[None, :, :] == rows[:, None, None],
        slot_weight.reshape(experts, capacity)[None, :, :],
        0.0,
    )
    routed = sum(
        jnp.einsum(
            "rec,ecd->rd",
            combine[:, :, lo:hi],
            part.astype(jnp.float32),
            precision=lax.Precision.HIGHEST,
            preferred_element_type=jnp.float32,
        )
        for lo, hi, part in zip(bounds[:-1], bounds[1:], returned)
    )

    group_rows = lax.all_gather(normed, "req", axis=0, tiled=True)
    s_gate = jnp.dot(group_rows, shared_gate, preferred_element_type=jnp.float32)
    s_up = jnp.dot(group_rows, shared_up, preferred_element_type=jnp.float32)
    s_hidden = (jax.nn.silu(s_gate) * s_up).astype(jnp.bfloat16)
    s_partial = lax.dot_general(
        s_hidden, shared_down, (((1,), (1,)), ((), ())), preferred_element_type=jnp.float32
    )
    shared = lax.psum_scatter(s_partial, "req", scatter_dimension=0, tiled=True)
    return (stream_f + routed + shared).astype(jnp.bfloat16)


def solution(mesh):
    return jax.shard_map(
        body,
        mesh=mesh,
        in_specs=(
            P(("req", "exp"), None),
            P(("req", "exp"), None),
            P("exp", None),
            P(),
            P(("req", "exp"), None),
            P(("req", "exp"), None),
            P("exp", None, None),
            P("exp", None, None),
            P("exp", None, None),
            P(None, "req"),
            P(None, "req"),
            P(None, "req"),
        ),
        out_specs=P(("req", "exp"), None),
        check_vma=False,
    )
```

```python
import jax
import jax.numpy as jnp
from jax import lax
from jax.sharding import PartitionSpec as P


def body(
    attn_out,
    residual,
    out_weight,
    norm_gain,
    expert_ids,
    gate_weights,
    expert_gate,
    expert_up,
    expert_down,
    shared_gate,
    shared_up,
    shared_down,
):
    row_count, width = attn_out.shape
    topk = expert_ids.shape[1]
    experts = lax.axis_size(EXP)
    capacity = min(row_count, 3 * row_count * topk // (2 * experts))
    core = lax.axis_index("core")
    cores = lax.axis_size("core")
    chip_rows = lax.all_gather(out_weight, "core", axis=0, tiled=True)
    cols = chip_rows.shape[1] // cores
    my_cols = lax.dynamic_slice_in_dim(chip_rows, core * cols, cols, 1)
    col_half = lax.all_gather(my_cols, "chip", axis=0, tiled=True)
    full_weight = lax.all_gather(col_half, "core", axis=1, tiled=True)
    proj = jnp.dot(attn_out, full_weight, preferred_element_type=jnp.float32)
    stream = (residual.astype(jnp.float32) + proj).astype(jnp.bfloat16)
    stream_f = stream.astype(jnp.float32)
    scale = lax.rsqrt(jnp.mean(stream_f * stream_f, axis=1, keepdims=True) + 1e-06)
    normed = (stream_f * scale * norm_gain).astype(jnp.bfloat16)

    flat_ids = expert_ids.reshape(-1)
    onehot = (flat_ids[:, None] == jnp.arange(experts, dtype=jnp.int32)[None, :]).astype(jnp.int32)
    position = jnp.sum(jnp.cumsum(onehot, axis=0) * onehot, axis=1) - 1
    slot = flat_ids * capacity + position
    source_row = jnp.arange(row_count * topk, dtype=jnp.int32) // topk
    table = jnp.full((experts * capacity,), row_count, jnp.int32).at[slot].set(source_row)
    rows = jnp.arange(row_count, dtype=jnp.int32)
    pick = (table.reshape(experts, capacity)[:, :, None] == rows[None, None, :]).astype(jnp.bfloat16)
    w_gate, w_up, w_down = expert_gate[0], expert_up[0], expert_down[0]
    bounds = [0, min(16, capacity), capacity] if capacity > 16 else [0, capacity]
    returned = []
    for lo, hi in zip(bounds[:-1], bounds[1:]):
        outgoing = jnp.einsum(
            "ecr,rd->ecd", pick[:, lo:hi], normed, preferred_element_type=jnp.float32
        ).astype(jnp.bfloat16)
        joined = lax.all_to_all(outgoing, EXP, split_axis=0, concat_axis=0, tiled=True)
        gate_part = jnp.einsum("scd,df->scf", joined, w_gate, preferred_element_type=jnp.float32)
        up_part = jnp.einsum("scd,df->scf", joined, w_up, preferred_element_type=jnp.float32)
        hidden = (jax.nn.silu(gate_part) * up_part).astype(jnp.bfloat16)
        result = jnp.einsum(
            "scf,fd->scd", hidden, w_down, preferred_element_type=jnp.float32
        ).astype(jnp.bfloat16)
        returned.append(lax.all_to_all(result, EXP, split_axis=0, concat_axis=0, tiled=True))
    slot_weight = jnp.zeros((experts * capacity,), jnp.float32).at[slot].set(gate_weights.reshape(-1))
    combine = jnp.where(
        table.reshape(experts, capacity)[None, :, :] == rows[:, None, None],
        slot_weight.reshape(experts, capacity)[None, :, :],
        0.0,
    )
    routed = sum(
        jnp.einsum(
            "rec,ecd->rd",
            combine[:, :, lo:hi],
            part.astype(jnp.float32),
            precision=lax.Precision.HIGHEST,
            preferred_element_type=jnp.float32,
        )
        for lo, hi, part in zip(bounds[:-1], bounds[1:], returned)
    )

    group_rows = lax.all_gather(normed, "req", axis=0, tiled=True)
    s_gate = jnp.dot(group_rows, shared_gate, preferred_element_type=jnp.float32)
    s_up = jnp.dot(group_rows, shared_up, preferred_element_type=jnp.float32)
    s_hidden = (jax.nn.silu(s_gate) * s_up).astype(jnp.bfloat16)
    s_partial = lax.dot_general(
        s_hidden, shared_down, (((1,), (1,)), ((), ())), preferred_element_type=jnp.float32
    )
    shared = lax.psum_scatter(s_partial, "req", scatter_dimension=0, tiled=True)
    return (stream_f + routed + shared).astype(jnp.bfloat16)


EXP = ("chip", "core")


def solution(mesh):
    req, exp = mesh.devices.shape
    chip_mesh = jax.sharding.Mesh(mesh.devices.reshape(req, exp // 2, 2), ("req", "chip", "core"))
    return jax.shard_map(
        body,
        mesh=chip_mesh,
        in_specs=(
            P(("req", "chip", "core"), None),
            P(("req", "chip", "core"), None),
            P(("chip", "core"), None),
            P(),
            P(("req", "chip", "core"), None),
            P(("req", "chip", "core"), None),
            P(("chip", "core"), None, None),
            P(("chip", "core"), None, None),
            P(("chip", "core"), None, None),
            P(None, "req"),
            P(None, "req"),
            P(None, "req"),
        ),
        out_specs=P(("req", "chip", "core"), None),
        check_vma=False,
    )
```

```python
import jax
import jax.numpy as jnp
from jax import lax
from jax.sharding import PartitionSpec as P


def body(
    attn_out,
    residual,
    out_weight,
    norm_gain,
    expert_ids,
    gate_weights,
    expert_gate,
    expert_up,
    expert_down,
    shared_gate,
    shared_up,
    shared_down,
):
    row_count, width = attn_out.shape
    topk = expert_ids.shape[1]
    experts = lax.axis_size("exp")
    capacity = min(row_count, 3 * row_count * topk // (2 * experts))
    flat_ids = expert_ids.reshape(-1)
    onehot = (flat_ids[:, None] == jnp.arange(experts, dtype=jnp.int32)[None, :]).astype(jnp.int32)
    position = jnp.sum(jnp.cumsum(onehot, axis=0) * onehot, axis=1) - 1
    slot = flat_ids * capacity + position
    source_row = jnp.arange(row_count * topk, dtype=jnp.int32) // topk
    table = jnp.full((experts * capacity,), row_count, jnp.int32).at[slot].set(source_row)
    rows = jnp.arange(row_count, dtype=jnp.int32)
    table, attn_out = lax.optimization_barrier((table, attn_out))
    proj = jnp.dot(
        attn_out,
        lax.all_gather(out_weight, "exp", axis=0, tiled=True),
        preferred_element_type=jnp.float32,
    )
    stream = (residual.astype(jnp.float32) + proj).astype(jnp.bfloat16)
    stream_f = stream.astype(jnp.float32)
    scale = lax.rsqrt(jnp.mean(stream_f * stream_f, axis=1, keepdims=True) + 1e-06)
    normed = (stream_f * scale * norm_gain).astype(jnp.bfloat16)

    pick = (table.reshape(experts, capacity)[:, :, None] == rows[None, None, :]).astype(jnp.bfloat16)
    w_gate, w_up, w_down = expert_gate[0], expert_up[0], expert_down[0]
    bounds = [0, min(16, capacity), capacity] if capacity > 16 else [0, capacity]
    returned = []
    for lo, hi in zip(bounds[:-1], bounds[1:]):
        outgoing = jnp.einsum(
            "ecr,rd->ecd", pick[:, lo:hi], normed, preferred_element_type=jnp.float32
        ).astype(jnp.bfloat16)
        joined = lax.all_to_all(outgoing, "exp", split_axis=0, concat_axis=0, tiled=True)
        gate_part = jnp.einsum("scd,df->scf", joined, w_gate, preferred_element_type=jnp.float32)
        up_part = jnp.einsum("scd,df->scf", joined, w_up, preferred_element_type=jnp.float32)
        hidden = (jax.nn.silu(gate_part) * up_part).astype(jnp.bfloat16)
        result = jnp.einsum(
            "scf,fd->scd", hidden, w_down, preferred_element_type=jnp.float32
        ).astype(jnp.bfloat16)
        returned.append(lax.all_to_all(result, "exp", split_axis=0, concat_axis=0, tiled=True))
    slot_weight = jnp.zeros((experts * capacity,), jnp.float32).at[slot].set(gate_weights.reshape(-1))
    combine = jnp.where(
        table.reshape(experts, capacity)[None, :, :] == rows[:, None, None],
        slot_weight.reshape(experts, capacity)[None, :, :],
        0.0,
    )
    combine_hi = combine.astype(jnp.bfloat16)
    combine_lo = (combine - combine_hi.astype(jnp.float32)).astype(jnp.bfloat16)
    routed = sum(
        jnp.einsum("rec,ecd->rd", weights[:, :, lo:hi], part, preferred_element_type=jnp.float32)
        for lo, hi, part in zip(bounds[:-1], bounds[1:], returned)
        for weights in (combine_hi, combine_lo)
    )

    group_rows = lax.all_gather(normed, "req", axis=0, tiled=True)
    s_gate = jnp.dot(group_rows, shared_gate, preferred_element_type=jnp.float32)
    s_up = jnp.dot(group_rows, shared_up, preferred_element_type=jnp.float32)
    s_hidden = (jax.nn.silu(s_gate) * s_up).astype(jnp.bfloat16)
    s_partial = lax.dot_general(
        s_hidden, shared_down, (((1,), (1,)), ((), ())), preferred_element_type=jnp.float32
    )
    shared = lax.psum_scatter(s_partial, "req", scatter_dimension=0, tiled=True)
    return (stream_f + routed + shared).astype(jnp.bfloat16)


def solution(mesh):
    return jax.shard_map(
        body,
        mesh=mesh,
        in_specs=(
            P(("req", "exp"), None),
            P(("req", "exp"), None),
            P("exp", None),
            P(),
            P(("req", "exp"), None),
            P(("req", "exp"), None),
            P("exp", None, None),
            P("exp", None, None),
            P("exp", None, None),
            P(None, "req"),
            P(None, "req"),
            P(None, "req"),
        ),
        out_specs=P(("req", "exp"), None),
        check_vma=False,
    )
```

```python
import jax
import jax.numpy as jnp
from jax import lax
from jax.sharding import PartitionSpec as P


def body(
    attn_out,
    residual,
    out_weight,
    norm_gain,
    expert_ids,
    gate_weights,
    expert_gate,
    expert_up,
    expert_down,
    shared_gate,
    shared_up,
    shared_down,
):
    row_count, width = attn_out.shape
    topk = expert_ids.shape[1]
    experts = lax.axis_size("exp")
    capacity = min(row_count, 3 * row_count * topk // (2 * experts))
    flat_ids = expert_ids.reshape(-1)
    onehot = (flat_ids[:, None] == jnp.arange(experts, dtype=jnp.int32)[None, :]).astype(jnp.int32)
    position = jnp.sum(jnp.cumsum(onehot, axis=0) * onehot, axis=1) - 1
    slot = flat_ids * capacity + position
    source_row = jnp.arange(row_count * topk, dtype=jnp.int32) // topk
    table = jnp.full((experts * capacity,), row_count, jnp.int32).at[slot].set(source_row)
    rows = jnp.arange(row_count, dtype=jnp.int32)
    table, attn_out = lax.optimization_barrier((table, attn_out))
    proj = jnp.dot(
        attn_out,
        lax.all_gather(out_weight, "exp", axis=0, tiled=True),
        preferred_element_type=jnp.float32,
    )
    stream = (residual.astype(jnp.float32) + proj).astype(jnp.bfloat16)
    stream_f = stream.astype(jnp.float32)
    scale = lax.rsqrt(jnp.mean(stream_f * stream_f, axis=1, keepdims=True) + 1e-06)
    normed = (stream_f * scale * norm_gain).astype(jnp.bfloat16)

    pick = (table.reshape(experts, capacity)[:, :, None] == rows[None, None, :]).astype(jnp.bfloat16)
    w_gate, w_up, w_down = expert_gate[0], expert_up[0], expert_down[0]
    bounds = [0, min(16, capacity), capacity] if capacity > 16 else [0, capacity]
    returned = []
    for lo, hi in zip(bounds[:-1], bounds[1:]):
        outgoing = jnp.einsum(
            "ecr,rd->ecd", pick[:, lo:hi], normed, preferred_element_type=jnp.float32
        ).astype(jnp.bfloat16)
        joined = lax.all_to_all(outgoing, "exp", split_axis=0, concat_axis=0, tiled=True)
        gate_part = jnp.einsum("scd,df->scf", joined, w_gate, preferred_element_type=jnp.float32)
        up_part = jnp.einsum("scd,df->scf", joined, w_up, preferred_element_type=jnp.float32)
        hidden = (jax.nn.silu(gate_part) * up_part).astype(jnp.bfloat16)
        result = jnp.einsum(
            "scf,fd->scd", hidden, w_down, preferred_element_type=jnp.float32
        ).astype(jnp.bfloat16)
        returned.append(lax.all_to_all(result, "exp", split_axis=0, concat_axis=0, tiled=True))
    slot_weight = jnp.zeros((experts * capacity,), jnp.float32).at[slot].set(gate_weights.reshape(-1))
    combine = jnp.where(
        table.reshape(experts, capacity)[None, :, :] == rows[:, None, None],
        slot_weight.reshape(experts, capacity)[None, :, :],
        0.0,
    )
    routed = sum(
        jnp.einsum(
            "rec,ecd->rd",
            combine[:, :, lo:hi],
            part.astype(jnp.float32),
            precision=lax.Precision.HIGHEST,
            preferred_element_type=jnp.float32,
        )
        for lo, hi, part in zip(bounds[:-1], bounds[1:], returned)
    )

    group_rows = lax.all_gather(normed, "req", axis=0, tiled=True)
    s_gate = jnp.dot(group_rows, shared_gate, preferred_element_type=jnp.float32)
    s_up = jnp.dot(group_rows, shared_up, preferred_element_type=jnp.float32)
    s_hidden = (jax.nn.silu(s_gate) * s_up).astype(jnp.bfloat16)
    s_partial = lax.dot_general(
        s_hidden, shared_down, (((1,), (1,)), ((), ())), preferred_element_type=jnp.float32
    )
    shared = lax.psum_scatter(s_partial, "req", scatter_dimension=0, tiled=True)
    return (stream_f + routed + shared).astype(jnp.bfloat16)


def solution(mesh):
    return jax.shard_map(
        body,
        mesh=mesh,
        in_specs=(
            P(("req", "exp"), None),
            P(("req", "exp"), None),
            P("exp", None),
            P(),
            P(("req", "exp"), None),
            P(("req", "exp"), None),
            P("exp", None, None),
            P("exp", None, None),
            P("exp", None, None),
            P(None, "req"),
            P(None, "req"),
            P(None, "req"),
        ),
        out_specs=P(("req", "exp"), None),
        check_vma=False,
    )
```

```python
import jax
import jax.numpy as jnp
from jax import lax
from jax.sharding import PartitionSpec as P


def body(
    attn_out,
    residual,
    out_weight,
    norm_gain,
    expert_ids,
    gate_weights,
    expert_gate,
    expert_up,
    expert_down,
    shared_gate,
    shared_up,
    shared_down,
):
    row_count, width = attn_out.shape
    topk = expert_ids.shape[1]
    experts = lax.axis_size("exp")
    capacity = min(row_count, 3 * row_count * topk // (2 * experts))
    flat_ids = expert_ids.reshape(-1)
    onehot = (flat_ids[:, None] == jnp.arange(experts, dtype=jnp.int32)[None, :]).astype(jnp.int32)
    position = jnp.sum(jnp.cumsum(onehot, axis=0) * onehot, axis=1) - 1
    slot = flat_ids * capacity + position
    source_row = jnp.arange(row_count * topk, dtype=jnp.int32) // topk
    table = jnp.full((experts * capacity,), row_count, jnp.int32).at[slot].set(source_row)
    rows = jnp.arange(row_count, dtype=jnp.int32)
    table, attn_out = lax.optimization_barrier((table, attn_out))
    proj = jnp.dot(
        attn_out,
        lax.all_gather(out_weight, "exp", axis=0, tiled=True),
        preferred_element_type=jnp.float32,
    )
    stream = (residual.astype(jnp.float32) + proj).astype(jnp.bfloat16)
    stream_f = stream.astype(jnp.float32)
    scale = lax.rsqrt(jnp.mean(stream_f * stream_f, axis=1, keepdims=True) + 1e-06)
    normed = (stream_f * scale * norm_gain).astype(jnp.bfloat16)

    pick = (table.reshape(experts, capacity)[:, :, None] == rows[None, None, :]).astype(jnp.bfloat16)
    w_gate, w_up, w_down = expert_gate[0], expert_up[0], expert_down[0]
    tail = min(16, capacity)
    bounds = [0, capacity - tail, capacity] if capacity > tail else [0, capacity]
    lanes = 128
    blocks = width // lanes
    returned = []
    landed = None
    for lo, hi in zip(bounds[:-1], bounds[1:]):
        size = hi - lo
        chunk_pick = pick[:, lo:hi]
        if landed is not None:
            chunk_pick, _ = lax.optimization_barrier((chunk_pick, landed))
        if size % 16:
            outgoing = jnp.einsum(
                "ecr,rjk->ecjk", chunk_pick, normed.reshape(row_count, blocks, lanes),
                preferred_element_type=jnp.float32,
            ).astype(jnp.bfloat16).reshape(experts, size * blocks, lanes)
            joined = lax.all_to_all(
                outgoing, "exp", split_axis=0, concat_axis=0, tiled=True
            ).reshape(experts, size, blocks, lanes)
            gate_part = jnp.einsum("scjk,jkf->scf", joined, w_gate.reshape(blocks, lanes, -1),
                                   preferred_element_type=jnp.float32)
            up_part = jnp.einsum("scjk,jkf->scf", joined, w_up.reshape(blocks, lanes, -1),
                                 preferred_element_type=jnp.float32)
        else:
            outgoing = jnp.einsum(
                "ecr,rd->ecd", chunk_pick, normed, preferred_element_type=jnp.float32
            ).astype(jnp.bfloat16)
            joined = lax.all_to_all(outgoing, "exp", split_axis=0, concat_axis=0, tiled=True)
            gate_part = jnp.einsum("scd,df->scf", joined, w_gate, preferred_element_type=jnp.float32)
            up_part = jnp.einsum("scd,df->scf", joined, w_up, preferred_element_type=jnp.float32)
        landed = joined
        hidden = (jax.nn.silu(gate_part) * up_part).astype(jnp.bfloat16)
        result = jnp.einsum(
            "scf,fd->scd", hidden, w_down, preferred_element_type=jnp.float32
        ).astype(jnp.bfloat16)
        if returned:
            result, _ = lax.optimization_barrier((result, returned[-1]))
        if size % 16:
            back = lax.all_to_all(
                result.reshape(experts, size * blocks, lanes), "exp",
                split_axis=0, concat_axis=0, tiled=True,
            )
            returned.append(back.reshape(experts, size, width))
        else:
            returned.append(lax.all_to_all(result, "exp", split_axis=0, concat_axis=0, tiled=True))
    slot_weight = jnp.zeros((experts * capacity,), jnp.float32).at[slot].set(gate_weights.reshape(-1))
    combine = jnp.where(
        table.reshape(experts, capacity)[None, :, :] == rows[:, None, None],
        slot_weight.reshape(experts, capacity)[None, :, :],
        0.0,
    )
    routed = sum(
        jnp.einsum(
            "rec,ecd->rd",
            combine[:, :, lo:hi],
            part.astype(jnp.float32),
            precision=lax.Precision.HIGHEST,
            preferred_element_type=jnp.float32,
        )
        for lo, hi, part in zip(bounds[:-1], bounds[1:], returned)
    )

    group_rows = lax.all_gather(normed, "req", axis=0, tiled=True)
    s_gate = jnp.dot(group_rows, shared_gate, preferred_element_type=jnp.float32)
    s_up = jnp.dot(group_rows, shared_up, preferred_element_type=jnp.float32)
    s_hidden = (jax.nn.silu(s_gate) * s_up).astype(jnp.bfloat16)
    s_partial = lax.dot_general(
        s_hidden, shared_down, (((1,), (1,)), ((), ())), preferred_element_type=jnp.float32
    )
    shared = lax.psum_scatter(s_partial, "req", scatter_dimension=0, tiled=True)
    return (stream_f + routed + shared).astype(jnp.bfloat16)


def solution(mesh):
    return jax.shard_map(
        body,
        mesh=mesh,
        in_specs=(
            P(("req", "exp"), None),
            P(("req", "exp"), None),
            P("exp", None),
            P(),
            P(("req", "exp"), None),
            P(("req", "exp"), None),
            P("exp", None, None),
            P("exp", None, None),
            P("exp", None, None),
            P(None, "req"),
            P(None, "req"),
            P(None, "req"),
        ),
        out_specs=P(("req", "exp"), None),
        check_vma=False,
    )
```

```python
import jax
import jax.numpy as jnp
from jax import lax
from jax.sharding import PartitionSpec as P


def body(
    attn_out,
    residual,
    out_weight,
    norm_gain,
    expert_ids,
    gate_weights,
    expert_gate,
    expert_up,
    expert_down,
    shared_gate,
    shared_up,
    shared_down,
):
    row_count, width = attn_out.shape
    topk = expert_ids.shape[1]
    experts = lax.axis_size("exp")
    capacity = min(row_count, 3 * row_count * topk // (2 * experts))
    flat_ids = expert_ids.reshape(-1)
    onehot = (flat_ids[:, None] == jnp.arange(experts, dtype=jnp.int32)[None, :]).astype(jnp.int32)
    position = jnp.sum(jnp.cumsum(onehot, axis=0) * onehot, axis=1) - 1
    slot = flat_ids * capacity + position
    source_row = jnp.arange(row_count * topk, dtype=jnp.int32) // topk
    table = jnp.full((experts * capacity,), row_count, jnp.int32).at[slot].set(source_row)
    rows = jnp.arange(row_count, dtype=jnp.int32)
    table, attn_out = lax.optimization_barrier((table, attn_out))
    proj = jnp.dot(
        attn_out,
        lax.all_gather(out_weight, "exp", axis=0, tiled=True),
        preferred_element_type=jnp.float32,
    )
    stream = (residual.astype(jnp.float32) + proj).astype(jnp.bfloat16)
    stream_f = stream.astype(jnp.float32)
    scale = lax.rsqrt(jnp.mean(stream_f * stream_f, axis=1, keepdims=True) + 1e-06)
    normed = (stream_f * scale * norm_gain).astype(jnp.bfloat16)

    pick = (table.reshape(experts, capacity)[:, :, None] == rows[None, None, :]).astype(jnp.bfloat16)
    w_gate, w_up, w_down = expert_gate[0], expert_up[0], expert_down[0]
    bounds = [0, capacity - 16, capacity] if capacity > 16 else [0, capacity]
    returned = []
    landed = None
    for lo, hi in zip(bounds[:-1], bounds[1:]):
        chunk_pick = pick[:, lo:hi]
        if landed is not None:
            chunk_pick, _ = lax.optimization_barrier((chunk_pick, landed))
        outgoing = jnp.einsum(
            "ecr,rd->ecd", chunk_pick, normed, preferred_element_type=jnp.float32
        ).astype(jnp.bfloat16)
        joined = lax.all_to_all(outgoing, "exp", split_axis=0, concat_axis=0, tiled=True)
        gate_part = jnp.einsum("scd,df->scf", joined, w_gate, preferred_element_type=jnp.float32)
        up_part = jnp.einsum("scd,df->scf", joined, w_up, preferred_element_type=jnp.float32)
        hidden = (jax.nn.silu(gate_part) * up_part).astype(jnp.bfloat16)
        result = jnp.einsum(
            "scf,fd->scd", hidden, w_down, preferred_element_type=jnp.float32
        ).astype(jnp.bfloat16)
        landed = joined
        if returned:
            result, _ = lax.optimization_barrier((result, returned[-1]))
        returned.append(lax.all_to_all(result, "exp", split_axis=0, concat_axis=0, tiled=True))
    slot_weight = jnp.zeros((experts * capacity,), jnp.float32).at[slot].set(gate_weights.reshape(-1))
    combine = jnp.where(
        table.reshape(experts, capacity)[None, :, :] == rows[:, None, None],
        slot_weight.reshape(experts, capacity)[None, :, :],
        0.0,
    )
    routed = sum(
        jnp.einsum(
            "rec,ecd->rd",
            combine[:, :, lo:hi],
            part.astype(jnp.float32),
            precision=lax.Precision.HIGHEST,
            preferred_element_type=jnp.float32,
        )
        for lo, hi, part in zip(bounds[:-1], bounds[1:], returned)
    )

    group_rows = lax.all_gather(normed, "req", axis=0, tiled=True)
    s_gate = jnp.dot(group_rows, shared_gate, preferred_element_type=jnp.float32)
    s_up = jnp.dot(group_rows, shared_up, preferred_element_type=jnp.float32)
    s_hidden = (jax.nn.silu(s_gate) * s_up).astype(jnp.bfloat16)
    s_partial = lax.dot_general(
        s_hidden, shared_down, (((1,), (1,)), ((), ())), preferred_element_type=jnp.float32
    )
    shared = lax.psum_scatter(s_partial, "req", scatter_dimension=0, tiled=True)
    return (stream_f + routed + shared).astype(jnp.bfloat16)


def solution(mesh):
    return jax.shard_map(
        body,
        mesh=mesh,
        in_specs=(
            P(("req", "exp"), None),
            P(("req", "exp"), None),
            P("exp", None),
            P(),
            P(("req", "exp"), None),
            P(("req", "exp"), None),
            P("exp", None, None),
            P("exp", None, None),
            P("exp", None, None),
            P(None, "req"),
            P(None, "req"),
            P(None, "req"),
        ),
        out_specs=P(("req", "exp"), None),
        check_vma=False,
    )
```

```python
import jax
import jax.numpy as jnp
from jax import lax
from jax.sharding import PartitionSpec as P


def body(
    attn_out,
    residual,
    out_weight,
    norm_gain,
    expert_ids,
    gate_weights,
    expert_gate,
    expert_up,
    expert_down,
    shared_gate,
    shared_up,
    shared_down,
):
    row_count, width = attn_out.shape
    topk = expert_ids.shape[1]
    experts = lax.axis_size("exp")
    capacity = min(row_count, 3 * row_count * topk // (2 * experts))
    flat_ids = expert_ids.reshape(-1)
    onehot = (flat_ids[:, None] == jnp.arange(experts, dtype=jnp.int32)[None, :]).astype(jnp.int32)
    position = jnp.sum(jnp.cumsum(onehot, axis=0) * onehot, axis=1) - 1
    slot = flat_ids * capacity + position
    source_row = jnp.arange(row_count * topk, dtype=jnp.int32) // topk
    table = jnp.full((experts * capacity,), row_count, jnp.int32).at[slot].set(source_row)
    rows = jnp.arange(row_count, dtype=jnp.int32)
    table, attn_out = lax.optimization_barrier((table, attn_out))
    proj = jnp.dot(
        attn_out,
        lax.all_gather(out_weight, "exp", axis=0, tiled=True),
        preferred_element_type=jnp.float32,
    )
    stream = (residual.astype(jnp.float32) + proj).astype(jnp.bfloat16)
    stream_f = stream.astype(jnp.float32)
    scale = lax.rsqrt(jnp.mean(stream_f * stream_f, axis=1, keepdims=True) + 1e-06)
    normed = (stream_f * scale * norm_gain).astype(jnp.bfloat16)

    pick = (table.reshape(experts, capacity)[:, :, None] == rows[None, None, :]).astype(jnp.bfloat16)
    w_gate, w_up, w_down = expert_gate[0], expert_up[0], expert_down[0]
    bounds = [0, min(16, capacity), capacity] if capacity > 16 else [0, capacity]
    returned = []
    for lo, hi in zip(bounds[:-1], bounds[1:]):
        outgoing = jnp.einsum(
            "ecr,rd->ecd", pick[:, lo:hi], normed, preferred_element_type=jnp.float32
        ).astype(jnp.bfloat16)
        joined = lax.all_to_all(outgoing, "exp", split_axis=0, concat_axis=0, tiled=True)
        gate_part = jnp.einsum("scd,df->scf", joined, w_gate, preferred_element_type=jnp.float32)
        up_part = jnp.einsum("scd,df->scf", joined, w_up, preferred_element_type=jnp.float32)
        hidden = (jax.nn.silu(gate_part) * up_part).astype(jnp.bfloat16)
        result = jnp.einsum(
            "scf,fd->scd", hidden, w_down, preferred_element_type=jnp.float32
        ).astype(jnp.bfloat16)
        returned.append(lax.all_to_all(result, "exp", split_axis=0, concat_axis=0, tiled=True))
    slot_weight = jnp.zeros((experts * capacity,), jnp.float32).at[slot].set(gate_weights.reshape(-1))
    combine = jnp.where(
        table.reshape(experts, capacity)[None, :, :] == rows[:, None, None],
        slot_weight.reshape(experts, capacity)[None, :, :],
        0.0,
    )
    routed = sum(
        jnp.einsum(
            "rec,ecd->rd",
            combine[:, :, lo:hi],
            part.astype(jnp.float32),
            precision=lax.Precision.HIGHEST,
            preferred_element_type=jnp.float32,
        )
        for lo, hi, part in zip(bounds[:-1], bounds[1:], returned)
    )

    req = lax.axis_size("req")
    me = lax.axis_index("req")
    shifted = [normed] + [
        lax.ppermute(normed, "req", perm=[(i, (i + k) % req) for i in range(req)])
        for k in range(1, req)
    ]
    order = (me - jnp.arange(req)) % req
    group_rows = jnp.take(jnp.stack(shifted), order, axis=0).reshape(req * row_count, width)
    s_gate = jnp.dot(group_rows, shared_gate, preferred_element_type=jnp.float32)
    s_up = jnp.dot(group_rows, shared_up, preferred_element_type=jnp.float32)
    s_hidden = (jax.nn.silu(s_gate) * s_up).astype(jnp.bfloat16)
    s_partial = lax.dot_general(
        s_hidden, shared_down, (((1,), (1,)), ((), ())), preferred_element_type=jnp.float32
    )
    shared = lax.psum_scatter(s_partial, "req", scatter_dimension=0, tiled=True)
    return (stream_f + routed + shared).astype(jnp.bfloat16)


def solution(mesh):
    return jax.shard_map(
        body,
        mesh=mesh,
        in_specs=(
            P(("req", "exp"), None),
            P(("req", "exp"), None),
            P("exp", None),
            P(),
            P(("req", "exp"), None),
            P(("req", "exp"), None),
            P("exp", None, None),
            P("exp", None, None),
            P("exp", None, None),
            P(None, "req"),
            P(None, "req"),
            P(None, "req"),
        ),
        out_specs=P(("req", "exp"), None),
        check_vma=False,
    )
```

```python
import jax
import jax.numpy as jnp
from jax import lax
from jax.sharding import PartitionSpec as P


def body(
    attn_out,
    residual,
    out_weight,
    norm_gain,
    expert_ids,
    gate_weights,
    expert_gate,
    expert_up,
    expert_down,
    shared_gate,
    shared_up,
    shared_down,
):
    row_count, width = attn_out.shape
    topk = expert_ids.shape[1]
    experts = lax.axis_size("exp")
    capacity = min(row_count, 3 * row_count * topk // (2 * experts))
    flat_ids = expert_ids.reshape(-1)
    onehot = (flat_ids[:, None] == jnp.arange(experts, dtype=jnp.int32)[None, :]).astype(jnp.int32)
    position = jnp.sum(jnp.cumsum(onehot, axis=0) * onehot, axis=1) - 1
    slot = flat_ids * capacity + position
    source_row = jnp.arange(row_count * topk, dtype=jnp.int32) // topk
    table = jnp.full((experts * capacity,), row_count, jnp.int32).at[slot].set(source_row)
    rows = jnp.arange(row_count, dtype=jnp.int32)
    table, attn_out = lax.optimization_barrier((table, attn_out))
    proj = jnp.dot(
        attn_out,
        lax.all_gather(out_weight, "exp", axis=0, tiled=True),
        preferred_element_type=jnp.float32,
    )
    stream = (residual.astype(jnp.float32) + proj).astype(jnp.bfloat16)
    stream_f = stream.astype(jnp.float32)
    scale = lax.rsqrt(jnp.mean(stream_f * stream_f, axis=1, keepdims=True) + 1e-06)
    normed = (stream_f * scale * norm_gain).astype(jnp.bfloat16)

    pick = (table.reshape(experts, capacity)[:, :, None] == rows[None, None, :]).astype(jnp.bfloat16)
    w_gate, w_up, w_down = expert_gate[0], expert_up[0], expert_down[0]
    bounds = [0, min(16, capacity), capacity] if capacity > 16 else [0, capacity]
    returned = []
    for lo, hi in zip(bounds[:-1], bounds[1:]):
        outgoing = jnp.einsum(
            "ecr,rd->ecd", pick[:, lo:hi], normed, preferred_element_type=jnp.float32
        ).astype(jnp.bfloat16)
        joined = lax.all_to_all(outgoing, "exp", split_axis=0, concat_axis=0, tiled=True)
        gate_part = jnp.einsum("scd,df->scf", joined, w_gate, preferred_element_type=jnp.float32)
        up_part = jnp.einsum("scd,df->scf", joined, w_up, preferred_element_type=jnp.float32)
        hidden = (jax.nn.silu(gate_part) * up_part).astype(jnp.bfloat16)
        result = jnp.einsum(
            "scf,fd->scd", hidden, w_down, preferred_element_type=jnp.float32
        ).astype(jnp.bfloat16)
        returned.append(lax.all_to_all(result, "exp", split_axis=0, concat_axis=0, tiled=True))
    slot_weight = jnp.zeros((experts * capacity,), jnp.float32).at[slot].set(gate_weights.reshape(-1))
    combine = jnp.where(
        table.reshape(experts, capacity)[None, :, :] == rows[:, None, None],
        slot_weight.reshape(experts, capacity)[None, :, :],
        0.0,
    )
    routed_parts = [
        jnp.einsum(
            "rec,ecd->rd",
            combine[:, :, lo:hi],
            part.astype(jnp.float32),
            precision=lax.Precision.HIGHEST,
            preferred_element_type=jnp.float32,
        )
        for lo, hi, part in zip(bounds[:-1], bounds[1:], returned)
    ]

    group_rows = lax.all_gather(normed, "req", axis=0, tiled=True)
    s_gate = jnp.dot(group_rows, shared_gate, preferred_element_type=jnp.float32)
    s_up = jnp.dot(group_rows, shared_up, preferred_element_type=jnp.float32)
    s_hidden = (jax.nn.silu(s_gate) * s_up).astype(jnp.bfloat16)
    s_partial = lax.dot_general(
        s_hidden, shared_down, (((1,), (1,)), ((), ())), preferred_element_type=jnp.float32
    )
    shared = lax.psum_scatter(s_partial, "req", scatter_dimension=0, tiled=True)
    ready = lax.optimization_barrier(stream_f + shared + sum(routed_parts[:-1]))
    return (ready + routed_parts[-1]).astype(jnp.bfloat16)


def solution(mesh):
    return jax.shard_map(
        body,
        mesh=mesh,
        in_specs=(
            P(("req", "exp"), None),
            P(("req", "exp"), None),
            P("exp", None),
            P(),
            P(("req", "exp"), None),
            P(("req", "exp"), None),
            P("exp", None, None),
            P("exp", None, None),
            P("exp", None, None),
            P(None, "req"),
            P(None, "req"),
            P(None, "req"),
        ),
        out_specs=P(("req", "exp"), None),
        check_vma=False,
    )
```

```python
import jax
import jax.numpy as jnp
from jax import lax
from jax.sharding import PartitionSpec as P


def body(
    attn_out,
    residual,
    out_weight,
    norm_gain,
    expert_ids,
    gate_weights,
    expert_gate,
    expert_up,
    expert_down,
    shared_gate,
    shared_up,
    shared_down,
):
    row_count, width = attn_out.shape
    topk = expert_ids.shape[1]
    experts = lax.axis_size("exp")
    capacity = min(row_count, 3 * row_count * topk // (2 * experts))
    flat_ids = expert_ids.reshape(-1)
    onehot = (flat_ids[:, None] == jnp.arange(experts, dtype=jnp.int32)[None, :]).astype(jnp.int32)
    position = jnp.sum(jnp.cumsum(onehot, axis=0) * onehot, axis=1) - 1
    slot = flat_ids * capacity + position
    source_row = jnp.arange(row_count * topk, dtype=jnp.int32) // topk
    table = jnp.full((experts * capacity,), row_count, jnp.int32).at[slot].set(source_row)
    rows = jnp.arange(row_count, dtype=jnp.int32)
    table, attn_out = lax.optimization_barrier((table, attn_out))
    proj = jnp.dot(
        attn_out,
        lax.all_gather(out_weight, "exp", axis=0, tiled=True),
        preferred_element_type=jnp.float32,
    )
    stream = (residual.astype(jnp.float32) + proj).astype(jnp.bfloat16)
    stream_f = stream.astype(jnp.float32)
    scale = lax.rsqrt(jnp.mean(stream_f * stream_f, axis=1, keepdims=True) + 1e-06)
    normed = (stream_f * scale * norm_gain).astype(jnp.bfloat16)

    pick = (table.reshape(experts, capacity)[:, :, None] == rows[None, None, :]).astype(jnp.bfloat16)
    w_gate, w_up, w_down = expert_gate[0], expert_up[0], expert_down[0]
    bounds = [0, min(16, capacity), capacity] if capacity > 16 else [0, capacity]
    returned = []
    for lo, hi in zip(bounds[:-1], bounds[1:]):
        outgoing = jnp.einsum(
            "ecr,rd->ecd", pick[:, lo:hi], normed, preferred_element_type=jnp.float32
        ).astype(jnp.bfloat16)
        joined = lax.all_to_all(outgoing, "exp", split_axis=0, concat_axis=0, tiled=True)
        gate_part = jnp.einsum("scd,df->scf", joined, w_gate, preferred_element_type=jnp.float32)
        up_part = jnp.einsum("scd,df->scf", joined, w_up, preferred_element_type=jnp.float32)
        hidden = (jax.nn.silu(gate_part) * up_part).astype(jnp.bfloat16)
        result = jnp.einsum(
            "scf,fd->scd", hidden, w_down, preferred_element_type=jnp.float32
        ).astype(jnp.bfloat16)
        returned.append(lax.all_to_all(result, "exp", split_axis=0, concat_axis=0, tiled=True))
    slot_weight = jnp.zeros((experts * capacity,), jnp.float32).at[slot].set(gate_weights.reshape(-1))
    combine = jnp.where(
        table.reshape(experts, capacity)[None, :, :] == rows[:, None, None],
        slot_weight.reshape(experts, capacity)[None, :, :],
        0.0,
    )
    routed = sum(
        jnp.einsum(
            "rec,ecd->rd",
            combine[:, :, lo:hi],
            part.astype(jnp.float32),
            precision=lax.Precision.HIGH,
            preferred_element_type=jnp.float32,
        )
        for lo, hi, part in zip(bounds[:-1], bounds[1:], returned)
    )

    group_rows = lax.all_gather(normed, "req", axis=0, tiled=True)
    s_gate = jnp.dot(group_rows, shared_gate, preferred_element_type=jnp.float32)
    s_up = jnp.dot(group_rows, shared_up, preferred_element_type=jnp.float32)
    s_hidden = (jax.nn.silu(s_gate) * s_up).astype(jnp.bfloat16)
    s_partial = lax.dot_general(
        s_hidden, shared_down, (((1,), (1,)), ((), ())), preferred_element_type=jnp.float32
    )
    shared = lax.psum_scatter(s_partial, "req", scatter_dimension=0, tiled=True)
    return (stream_f + routed + shared).astype(jnp.bfloat16)


def solution(mesh):
    return jax.shard_map(
        body,
        mesh=mesh,
        in_specs=(
            P(("req", "exp"), None),
            P(("req", "exp"), None),
            P("exp", None),
            P(),
            P(("req", "exp"), None),
            P(("req", "exp"), None),
            P("exp", None, None),
            P("exp", None, None),
            P("exp", None, None),
            P(None, "req"),
            P(None, "req"),
            P(None, "req"),
        ),
        out_specs=P(("req", "exp"), None),
        check_vma=False,
    )
```

```python
import jax
import jax.numpy as jnp
from jax import lax
from jax.sharding import PartitionSpec as P


def body(
    attn_out,
    residual,
    out_weight,
    norm_gain,
    expert_ids,
    gate_weights,
    expert_gate,
    expert_up,
    expert_down,
    shared_gate,
    shared_up,
    shared_down,
):
    row_count, width = attn_out.shape
    topk = expert_ids.shape[1]
    experts = lax.axis_size("exp")
    capacity = min(row_count, 3 * row_count * topk // (2 * experts))
    flat_ids = expert_ids.reshape(-1)
    onehot = (flat_ids[:, None] == jnp.arange(experts, dtype=jnp.int32)[None, :]).astype(jnp.int32)
    position = jnp.sum(jnp.cumsum(onehot, axis=0) * onehot, axis=1) - 1
    slot = flat_ids * capacity + position
    source_row = jnp.arange(row_count * topk, dtype=jnp.int32) // topk
    table = jnp.full((experts * capacity,), row_count, jnp.int32).at[slot].set(source_row)
    rows = jnp.arange(row_count, dtype=jnp.int32)
    table, attn_out = lax.optimization_barrier((table, attn_out))
    proj = jnp.dot(
        attn_out,
        lax.all_gather(out_weight, "exp", axis=0, tiled=True),
        preferred_element_type=jnp.float32,
    )
    proj = lax.optimization_barrier(proj)
    stream = (residual.astype(jnp.float32) + proj).astype(jnp.bfloat16)
    stream_f = stream.astype(jnp.float32)
    scale = lax.rsqrt(jnp.mean(stream_f * stream_f, axis=1, keepdims=True) + 1e-06)
    normed = (stream_f * scale * norm_gain).astype(jnp.bfloat16)

    pick = (table.reshape(experts, capacity)[:, :, None] == rows[None, None, :]).astype(jnp.bfloat16)
    w_gate, w_up, w_down = expert_gate[0], expert_up[0], expert_down[0]
    bounds = [0, min(16, capacity), capacity] if capacity > 16 else [0, capacity]
    returned = []
    for lo, hi in zip(bounds[:-1], bounds[1:]):
        outgoing = jnp.einsum(
            "ecr,rd->ecd", pick[:, lo:hi], normed, preferred_element_type=jnp.float32
        ).astype(jnp.bfloat16)
        joined = lax.all_to_all(outgoing, "exp", split_axis=0, concat_axis=0, tiled=True)
        gate_part = jnp.einsum("scd,df->scf", joined, w_gate, preferred_element_type=jnp.float32)
        up_part = jnp.einsum("scd,df->scf", joined, w_up, preferred_element_type=jnp.float32)
        hidden = (jax.nn.silu(gate_part) * up_part).astype(jnp.bfloat16)
        result = jnp.einsum(
            "scf,fd->scd", hidden, w_down, preferred_element_type=jnp.float32
        ).astype(jnp.bfloat16)
        returned.append(lax.all_to_all(result, "exp", split_axis=0, concat_axis=0, tiled=True))
    slot_weight = jnp.zeros((experts * capacity,), jnp.float32).at[slot].set(gate_weights.reshape(-1))
    combine = jnp.where(
        table.reshape(experts, capacity)[None, :, :] == rows[:, None, None],
        slot_weight.reshape(experts, capacity)[None, :, :],
        0.0,
    )
    routed = sum(
        jnp.einsum(
            "rec,ecd->rd",
            combine[:, :, lo:hi],
            part.astype(jnp.float32),
            precision=lax.Precision.HIGH,
            preferred_element_type=jnp.float32,
        )
        for lo, hi, part in zip(bounds[:-1], bounds[1:], returned)
    )

    group_rows = lax.all_gather(normed, "req", axis=0, tiled=True)
    s_gate = jnp.dot(group_rows, shared_gate, preferred_element_type=jnp.float32)
    s_up = jnp.dot(group_rows, shared_up, preferred_element_type=jnp.float32)
    s_hidden = (jax.nn.silu(s_gate) * s_up).astype(jnp.bfloat16)
    s_partial = lax.dot_general(
        s_hidden, shared_down, (((1,), (1,)), ((), ())), preferred_element_type=jnp.float32
    )
    shared = lax.psum_scatter(s_partial, "req", scatter_dimension=0, tiled=True)
    return (stream_f + routed + shared).astype(jnp.bfloat16)


def solution(mesh):
    return jax.shard_map(
        body,
        mesh=mesh,
        in_specs=(
            P(("req", "exp"), None),
            P(("req", "exp"), None),
            P("exp", None),
            P(),
            P(("req", "exp"), None),
            P(("req", "exp"), None),
            P("exp", None, None),
            P("exp", None, None),
            P("exp", None, None),
            P(None, "req"),
            P(None, "req"),
            P(None, "req"),
        ),
        out_specs=P(("req", "exp"), None),
        check_vma=False,
    )
```

```python
import jax
import jax.numpy as jnp
from jax import lax
from jax.sharding import PartitionSpec as P


def body(
    attn_out,
    residual,
    out_weight,
    norm_gain,
    expert_ids,
    gate_weights,
    expert_gate,
    expert_up,
    expert_down,
    shared_gate,
    shared_up,
    shared_down,
):
    row_count, width = attn_out.shape
    topk = expert_ids.shape[1]
    experts = lax.axis_size("exp")
    capacity = min(row_count, 3 * row_count * topk // (2 * experts))
    flat_ids = expert_ids.reshape(-1)
    onehot = (flat_ids[:, None] == jnp.arange(experts, dtype=jnp.int32)[None, :]).astype(jnp.int32)
    position = jnp.sum(jnp.cumsum(onehot, axis=0) * onehot, axis=1) - 1
    slot = flat_ids * capacity + position
    source_row = jnp.arange(row_count * topk, dtype=jnp.int32) // topk
    table = jnp.full((experts * capacity,), row_count, jnp.int32).at[slot].set(source_row)
    rows = jnp.arange(row_count, dtype=jnp.int32)
    table, attn_out = lax.optimization_barrier((table, attn_out))
    proj = jnp.dot(
        attn_out,
        lax.all_gather(out_weight, "exp", axis=0, tiled=True),
        preferred_element_type=jnp.float32,
    )
    proj = lax.optimization_barrier(proj)
    stream = (residual.astype(jnp.float32) + proj).astype(jnp.bfloat16)
    stream_f = stream.astype(jnp.float32)
    scale = lax.rsqrt(jnp.mean(stream_f * stream_f, axis=1, keepdims=True) + 1e-06)
    normed = (stream_f * scale * norm_gain).astype(jnp.bfloat16)

    pick = (table.reshape(experts, capacity)[:, :, None] == rows[None, None, :]).astype(jnp.bfloat16)
    w_gate, w_up, w_down = expert_gate[0], expert_up[0], expert_down[0]
    bounds = [0, min(16, capacity), capacity] if capacity > 16 else [0, capacity]
    returned = []
    for lo, hi in zip(bounds[:-1], bounds[1:]):
        padded = jnp.concatenate([normed, jnp.zeros((1, width), jnp.bfloat16)], axis=0)
        outgoing = padded[table.reshape(experts, capacity)[:, lo:hi]]
        joined = lax.all_to_all(outgoing, "exp", split_axis=0, concat_axis=0, tiled=True)
        gate_part = jnp.einsum("scd,df->scf", joined, w_gate, preferred_element_type=jnp.float32)
        up_part = jnp.einsum("scd,df->scf", joined, w_up, preferred_element_type=jnp.float32)
        hidden = (jax.nn.silu(gate_part) * up_part).astype(jnp.bfloat16)
        result = jnp.einsum(
            "scf,fd->scd", hidden, w_down, preferred_element_type=jnp.float32
        ).astype(jnp.bfloat16)
        returned.append(lax.all_to_all(result, "exp", split_axis=0, concat_axis=0, tiled=True))
    slots = jnp.arange(experts * capacity, dtype=jnp.int32)
    row_slots = slot.reshape(row_count, topk)
    combine = jnp.sum(
        jnp.where(row_slots[:, :, None] == slots[None, None, :], gate_weights[:, :, None], 0.0),
        axis=1,
    ).reshape(row_count, experts, capacity)
    routed = sum(
        jnp.einsum(
            "rec,ecd->rd",
            combine[:, :, lo:hi],
            part.astype(jnp.float32),
            precision=lax.Precision.HIGH,
            preferred_element_type=jnp.float32,
        )
        for lo, hi, part in zip(bounds[:-1], bounds[1:], returned)
    )

    group_rows = lax.all_gather(normed, "req", axis=0, tiled=True)
    s_gate = jnp.dot(group_rows, shared_gate, preferred_element_type=jnp.float32)
    s_up = jnp.dot(group_rows, shared_up, preferred_element_type=jnp.float32)
    s_hidden = (jax.nn.silu(s_gate) * s_up).astype(jnp.bfloat16)
    s_partial = lax.dot_general(
        s_hidden, shared_down, (((1,), (1,)), ((), ())), preferred_element_type=jnp.float32
    )
    shared = lax.psum_scatter(s_partial, "req", scatter_dimension=0, tiled=True)
    return (stream_f + routed + shared).astype(jnp.bfloat16)


def solution(mesh):
    return jax.shard_map(
        body,
        mesh=mesh,
        in_specs=(
            P(("req", "exp"), None),
            P(("req", "exp"), None),
            P("exp", None),
            P(),
            P(("req", "exp"), None),
            P(("req", "exp"), None),
            P("exp", None, None),
            P("exp", None, None),
            P("exp", None, None),
            P(None, "req"),
            P(None, "req"),
            P(None, "req"),
        ),
        out_specs=P(("req", "exp"), None),
        check_vma=False,
    )
```

```python
import jax
import jax.numpy as jnp
from jax import lax
from jax.sharding import PartitionSpec as P


def body(
    attn_out,
    residual,
    out_weight,
    norm_gain,
    expert_ids,
    gate_weights,
    expert_gate,
    expert_up,
    expert_down,
    shared_gate,
    shared_up,
    shared_down,
):
    row_count, width = attn_out.shape
    topk = expert_ids.shape[1]
    experts = lax.axis_size("exp")
    capacity = min(row_count, 3 * row_count * topk // (2 * experts))
    flat_ids = expert_ids.reshape(-1)
    onehot = (flat_ids[:, None] == jnp.arange(experts, dtype=jnp.int32)[None, :]).astype(jnp.int32)
    position = jnp.sum(jnp.cumsum(onehot, axis=0) * onehot, axis=1) - 1
    slot = flat_ids * capacity + position
    source_row = jnp.arange(row_count * topk, dtype=jnp.int32) // topk
    table = jnp.full((experts * capacity,), row_count, jnp.int32).at[slot].set(source_row)
    rows = jnp.arange(row_count, dtype=jnp.int32)
    table, attn_out = lax.optimization_barrier((table, attn_out))
    proj = jnp.dot(
        attn_out,
        lax.all_gather(out_weight, "exp", axis=0, tiled=True),
        preferred_element_type=jnp.float32,
    )
    proj = lax.optimization_barrier(proj)
    stream = (residual.astype(jnp.float32) + proj).astype(jnp.bfloat16)
    stream_f = stream.astype(jnp.float32)
    scale = lax.rsqrt(jnp.mean(stream_f * stream_f, axis=1, keepdims=True) + 1e-06)
    normed = (stream_f * scale * norm_gain).astype(jnp.bfloat16)

    pick = (table.reshape(experts, capacity)[:, :, None] == rows[None, None, :]).astype(jnp.bfloat16)
    w_gate, w_up, w_down = expert_gate[0], expert_up[0], expert_down[0]
    bounds = [0, min(16, capacity), capacity] if capacity > 16 else [0, capacity]
    returned = []
    for lo, hi in zip(bounds[:-1], bounds[1:]):
        outgoing = jnp.einsum(
            "ecr,rd->ecd", pick[:, lo:hi], normed, preferred_element_type=jnp.float32
        ).astype(jnp.bfloat16)
        joined = lax.all_to_all(outgoing, "exp", split_axis=0, concat_axis=0, tiled=True)
        if lo == 0:
            first_landed = joined
        gate_part = jnp.einsum("scd,df->scf", joined, w_gate, preferred_element_type=jnp.float32)
        up_part = jnp.einsum("scd,df->scf", joined, w_up, preferred_element_type=jnp.float32)
        hidden = (jax.nn.silu(gate_part) * up_part).astype(jnp.bfloat16)
        result = jnp.einsum(
            "scf,fd->scd", hidden, w_down, preferred_element_type=jnp.float32
        ).astype(jnp.bfloat16)
        returned.append(lax.all_to_all(result, "exp", split_axis=0, concat_axis=0, tiled=True))
    slot_weight = jnp.zeros((experts * capacity,), jnp.float32).at[slot].set(gate_weights.reshape(-1))
    combine = jnp.where(
        table.reshape(experts, capacity)[None, :, :] == rows[:, None, None],
        slot_weight.reshape(experts, capacity)[None, :, :],
        0.0,
    )
    routed = sum(
        jnp.einsum(
            "rec,ecd->rd",
            combine[:, :, lo:hi],
            part.astype(jnp.float32),
            precision=lax.Precision.HIGH,
            preferred_element_type=jnp.float32,
        )
        for lo, hi, part in zip(bounds[:-1], bounds[1:], returned)
    )

    group_rows = lax.all_gather(normed, "req", axis=0, tiled=True)
    group_rows, _ = lax.optimization_barrier((group_rows, first_landed))
    s_gate = jnp.dot(group_rows, shared_gate, preferred_element_type=jnp.float32)
    s_up = jnp.dot(group_rows, shared_up, preferred_element_type=jnp.float32)
    s_hidden = (jax.nn.silu(s_gate) * s_up).astype(jnp.bfloat16)
    s_partial = lax.dot_general(
        s_hidden, shared_down, (((1,), (1,)), ((), ())), preferred_element_type=jnp.float32
    )
    shared = lax.psum_scatter(s_partial, "req", scatter_dimension=0, tiled=True)
    return (stream_f + routed + shared).astype(jnp.bfloat16)


def solution(mesh):
    return jax.shard_map(
        body,
        mesh=mesh,
        in_specs=(
            P(("req", "exp"), None),
            P(("req", "exp"), None),
            P("exp", None),
            P(),
            P(("req", "exp"), None),
            P(("req", "exp"), None),
            P("exp", None, None),
            P("exp", None, None),
            P("exp", None, None),
            P(None, "req"),
            P(None, "req"),
            P(None, "req"),
        ),
        out_specs=P(("req", "exp"), None),
        check_vma=False,
    )
```
